32 devices in a mesh: blk: 8 (over z, y), head: 4 (over x, core).
Axes of the slice: x: 2, y: 2, z: 4, core: 2. Of those that a mesh axis runs over, the one named last changes fastest.
Arguments:
- queries: bfloat16 [4096, 1024], P('blk', 'head'), may hold values from -170 to 170
- key_rows: bfloat16 [4096, 1024], P('blk', 'head'), may hold values from -9 to 9
- values: bfloat16 [4096, 1024], P('blk', 'head'), may hold values from -48 to 48
- text_keys: bfloat16 [308, 1024], P(None, 'head'), may hold values from -9 to 9
- text_values: bfloat16 [308, 1024], P(None, 'head'), may hold values from -48 to 48
- block_image: int32 [32], replicated, may hold values from 0 to 1, as said below
- gate_image: float32 [2, 1536], replicated, may hold values from 0.5 to 2
- residual: bfloat16 [4096, 1536], P(('blk', 'head')), may hold values from -6 to 6
- w_out: bfloat16 [1024, 1536], P('head'), may hold values from -0.1875 to 0.1875
Outputs:
- stream_out: bfloat16 [4096, 1536], P(('blk', 'head'))
The draws below stay inside these ranges and needn't reach their ends.
Inputs may be any that keep to these rules, and one draw needn't show every extreme that they name: `block_image`: each image number 0 to 1 names 8 to 24 of the entries, some image exactly 24 and some exactly 8; the blocks of an image lie anywhere in the array.
All inputs are finite; a program needn't handle non-finite values.
Results may differ from the reference program's by a relative error of at most 0.014.
Values may be sent and summed in bfloat16 or wider, within the bound.
No kernel may reach another device: no remote copies, remote signals or barrier semaphores. Data moves between devices by JAX's collectives and lax.ppermute only.
A program may use at most 64 MiB of HBM per device.

```python
import math
import jax
import jax.numpy as jnp
from jax import lax

D = 1536
HEADS = 16
HD = 64
TEXT = 154
BS = 128
TOK_BLK = 512
NBLOCKS = 32
IMAGES = 2
TOKENS = 4096


def shared_keys(key):
    base = 1.5 * jax.random.normal(jax.random.fold_in(key, 7), (TOKENS, HEADS * HD), jnp.float32)
    base = jnp.clip(base, -9.0, 9.0)
    return base


def draw_key_rows(key, part):
    base = shared_keys(key)
    return base.astype(jnp.bfloat16)


def draw_queries(key, part):
    fresh = 1.5 * jax.random.normal(jax.random.fold_in(key, 9), (TOKENS, HEADS * HD), jnp.float32)
    fresh = jnp.clip(fresh, -9.0, 9.0)
    return fresh.astype(jnp.bfloat16)


def draw_block_image(key, part):
    pairs = IMAGES // 2
    split = jax.random.randint(jax.random.fold_in(key, 1), (pairs,), 8, 25)
    split = split.at[0].set(24)
    counts = jnp.stack([split, 32 - split], axis=1).reshape(IMAGES)
    labels = jax.random.permutation(jax.random.fold_in(key, 2), IMAGES).astype(jnp.int32)
    bounds = jnp.cumsum(counts)
    blocks = jnp.arange(NBLOCKS)
    sorted_slot = jnp.sum((blocks[:, None] >= bounds[None, :]).astype(jnp.int32), axis=1)
    image = labels[sorted_slot]
    order = jax.random.permutation(jax.random.fold_in(key, 3), NBLOCKS)
    return image[order].astype(jnp.int32)


def shard_levels(key, extent, shards, smallest, high):
    loudness = 1.0
    for position, blocks in shards:
        steps = jax.random.uniform(jax.random.fold_in(jax.random.fold_in(key, 6), position), (blocks,), jnp.float32, smallest / len(shards), high / len(shards))
        loudness = loudness * jnp.repeat(jnp.exp(steps), extent[position] // blocks).reshape((-1,) + (1,) * (len(extent) - 1 - position))
    return loudness


def centred(rng, extent, spread, reach, cuts=(), kind=jnp.bfloat16):
    values = spread * jax.random.normal(rng, extent, jnp.float32)
    if cuts:
        values = values * shard_levels(rng, extent, cuts, -0.22, 0.18)
    return jnp.clip(values, -reach, reach).astype(kind)


def setup_inputs(seed: int = 0) -> dict:
    splits = jax.random.split(jax.random.key(seed), 10)
    queries = draw_queries(jax.random.fold_in(splits[9], 71), 0)
    key_rows = draw_key_rows(jax.random.fold_in(splits[9], 71), 0)
    values = centred(splits[2], (TOKENS, HEADS * HD), 8.0, 48.0, ((0, 8), (1, 4)))
    text_keys = centred(splits[3], (IMAGES * TEXT, HEADS * HD), 1.5, 9.0, ((1, 4),))
    text_values = centred(splits[4], (IMAGES * TEXT, HEADS * HD), 8.0, 48.0, ((1, 4),))
    block_image = draw_block_image(jax.random.fold_in(splits[9], 71), 0)
    gate_image = jnp.clip(jax.random.uniform(splits[6], (IMAGES, D), jnp.float32, 0.5, 2.0), 0.5, 2.0)
    residual = centred(splits[7], (TOKENS, D), 1.0, 6.0, ((0, 32),))
    w_out = centred(splits[8], (HEADS * HD, D), (HEADS * HD) ** -0.5, 0.1875, ((0, 4),))
    return dict(queries=queries, key_rows=key_rows, values=values, text_keys=text_keys, text_values=text_values, block_image=block_image, gate_image=gate_image, residual=residual, w_out=w_out)


def reference(queries, key_rows, values, text_keys, text_values, block_image, gate_image, residual, w_out):
    token_image = jnp.repeat(block_image, BS).astype(jnp.int32)
    text_image = (jnp.arange(IMAGES * TEXT) // TEXT).astype(jnp.int32)
    every_key = jnp.concatenate([key_rows, text_keys], axis=0)
    every_value = jnp.concatenate([values, text_values], axis=0)
    key_image = jnp.concatenate([token_image, text_image], axis=0)
    scale = 1.0 / math.sqrt(HD)
    nkeys = every_key.shape[0]
    query_heads = queries.reshape(TOKENS, HEADS, HD).transpose(1, 0, 2)
    key_heads = every_key.reshape(nkeys, HEADS, HD).transpose(1, 0, 2)
    value_heads = every_value.reshape(nkeys, HEADS, HD).transpose(1, 0, 2)
    query_blocks = query_heads.reshape(HEADS, TOKENS // TOK_BLK, TOK_BLK, HD)
    image_blocks = token_image.reshape(TOKENS // TOK_BLK, TOK_BLK)

    def one_head(operands):
        qhead, khead, vhead = operands

        def one_block(inner):
            qblock, qimage = inner
            scores = jnp.dot(qblock, khead.T, preferred_element_type=jnp.float32) * scale
            allowed = qimage[:, None] == key_image[None, :]
            scores = jnp.where(allowed, scores, -1e+30)
            peak = lax.optimization_barrier(jnp.max(scores, axis=1, keepdims=True))
            expo = jnp.exp(scores - peak)
            denom = lax.optimization_barrier(jnp.sum(expo, axis=1, keepdims=True))
            numer = jnp.dot(expo.astype(jnp.bfloat16), vhead, preferred_element_type=jnp.float32)
            return (numer / denom).astype(jnp.bfloat16)
        return lax.map(one_block, (qhead, image_blocks))
    attended = lax.map(one_head, (query_blocks, key_heads, value_heads))
    attended = attended.reshape(HEADS, TOKENS, HD).transpose(1, 0, 2).reshape(TOKENS, HEADS * HD)
    projected = jnp.dot(attended, w_out, preferred_element_type=jnp.float32)
    gating = gate_image[token_image]
    return (residual.astype(jnp.float32) + gating * projected).astype(jnp.bfloat16)
```

```python
import math

import jax
import jax.numpy as jnp
from jax import lax
from jax.experimental import pallas as pl
from jax.experimental.pallas import tpu as pltpu
from jax.sharding import PartitionSpec as P

HD = 64
TEXT = 154
BS = 128
GROUP = 4
WIDE = 8


neg_large = -1e30


def absorb(running, query_three, query_image, key_slab, value_slab, key_image):
    best, total, accum = running
    heads = query_three.shape[1]
    width = query_three.shape[2]
    key_three = key_slab.reshape(key_slab.shape[0], heads, width)
    value_three = value_slab.reshape(value_slab.shape[0], heads, width)
    scores = jnp.einsum("qhd,khd->hqk", query_three, key_three, preferred_element_type=jnp.float32)
    scores = scores * (1.0 / math.sqrt(width))
    allowed = query_image[:, None] == key_image[None, :]
    scores = jnp.where(allowed[None], scores, neg_large)
    newbest = jnp.maximum(best, jnp.max(scores, axis=2))
    weights = jnp.exp(scores - newbest[..., None])
    shrink = jnp.exp(best - newbest)
    total = total * shrink + jnp.sum(weights, axis=2)
    update = jnp.einsum(
        "hqk,khd->hqd",
        weights.astype(jnp.bfloat16),
        value_three,
        preferred_element_type=jnp.float32,
    )
    accum = accum * shrink[..., None] + update
    return (newbest, total, accum)


def on_device(
    queries, key_rows, values, text_keys, text_values, block_image, gate_image, residual, w_out
):
    tok_blk = queries.shape[0]
    ncols = queries.shape[1]
    heads_here = ncols // HD
    blocks_here = tok_blk // BS
    token_image = jnp.repeat(block_image, BS)
    blk_index = lax.axis_index("blk")
    my_blocks = lax.dynamic_slice_in_dim(block_image, blk_index * blocks_here, blocks_here)
    query_image = jnp.repeat(my_blocks, BS)
    text_image = jnp.arange(text_keys.shape[0]) // TEXT
    start_state = (
        jnp.full((heads_here, tok_blk), neg_large, jnp.float32),
        jnp.zeros((heads_here, tok_blk), jnp.float32),
        jnp.zeros((heads_here, tok_blk, HD), jnp.float32),
    )
    query_three = queries.reshape(tok_blk, heads_here, HD)
    running = absorb(start_state, query_three, query_image, text_keys, text_values, text_image)
    fold_running = running
    key_piece = lax.all_gather(key_rows, "blk", axis=0, tiled=True)
    value_piece = lax.all_gather(values, "blk", axis=0, tiled=True)
    length = key_piece.shape[0]

    def advance(state, position):
        begin = position * tok_blk
        key_slab = lax.dynamic_slice_in_dim(key_piece, begin, tok_blk)
        value_slab = lax.dynamic_slice_in_dim(value_piece, begin, tok_blk)
        slab_image = lax.dynamic_slice_in_dim(token_image, begin, tok_blk)
        return (absorb(state, query_three, query_image, key_slab, value_slab, slab_image), None)

    fold_running, unused = lax.scan(
        advance, fold_running, jnp.arange(length // tok_blk, dtype=jnp.int32)
    )
    best, total, accum = fold_running
    attended = (accum / total[..., None]).astype(jnp.bfloat16)
    attended = attended.transpose(1, 0, 2).reshape(tok_blk, ncols)
    tok_dev = tok_blk // lax.axis_size("head")
    mixed = lax.all_to_all(attended, "head", split_axis=0, concat_axis=1, tiled=True)
    projected = jnp.dot(
        mixed, lax.all_gather(w_out, "head", axis=0, tiled=True), preferred_element_type=jnp.float32
    )
    head_index = lax.axis_index("head")
    row_image = lax.dynamic_slice_in_dim(query_image, head_index * tok_dev, tok_dev)
    onehot = (
        row_image[:, None] == jnp.arange(gate_image.shape[0], dtype=jnp.int32)[None, :]
    ).astype(jnp.float32)
    gating = jnp.dot(onehot, gate_image, precision=lax.Precision.HIGHEST)
    return (residual.astype(jnp.float32) + gating * projected).astype(jnp.bfloat16)

def round_up(count, unit):
    return -(-count // unit) * unit


def pack_kernel(head_ref, q_ref, k_ref, v_ref, tk_ref, tv_ref, send_ref, text_ref):
    heads = q_ref.shape[1] // HD
    parts = send_ref.shape[0] // heads
    rows = q_ref.shape[0]
    blocks = rows // BS
    share = BS // parts
    for h in range(heads):
        cols = slice(h * HD, (h + 1) * HD)
        pair = jnp.concatenate([k_ref[:, cols], v_ref[:, cols]], axis=1)
        for r in range(parts):
            send_ref[h * parts + r, 0:rows, :] = pair
            for i in range(blocks // 2):
                low = i * BS + r * share
                high = (i + blocks // 2) * BS + r * share
                send_ref[h * parts + r, rows + i * share : rows + (i + 1) * share, :] = (
                    jnp.concatenate(
                        [q_ref[low : low + share, cols], q_ref[high : high + share, cols]], axis=1
                    )
                )
    ntext = tk_ref.shape[0]
    text_ref[...] = jnp.zeros(text_ref.shape, text_ref.dtype)
    for h in range(heads):

        @pl.when(head_ref[0] == h)
        def _():
            cols = slice(h * HD, (h + 1) * HD)
            text_ref[0:ntext, :] = jnp.concatenate([tk_ref[:, cols], tv_ref[:, cols]], axis=1)


def attend_kernel(
    image_ref, got_ref, text_ref, out_ref, keys_ref, vals_ref, q_ref, o_ref, start_ref, count_ref, pos_ref
):
    nblocks = image_ref.shape[0]
    images = count_ref.shape[0]
    sources = got_ref.shape[0]
    per = nblocks // sources
    rows = per * BS
    share = out_ref.shape[1] * 2
    exponent = math.log2(math.e) / math.sqrt(HD)
    for i in range(images):
        count_ref[i] = 0

    def tally(j, carry):
        image = image_ref[j]
        count_ref[image] = count_ref[image] + 1
        return carry

    lax.fori_loop(0, nblocks, tally, 0)
    begin = jnp.int32(0)
    for i in range(images):
        start_ref[i] = begin
        begin = begin + count_ref[i]

    def place(b, carry):
        for i in range(per):
            image = image_ref[b * per + i]
            spot = start_ref[image]
            start_ref[image] = spot + 1
            pos_ref[b * per + i] = spot
            block = got_ref[b, i * BS : (i + 1) * BS, :]
            keys_ref[pl.ds(pl.multiple_of(spot * BS, BS), BS), :] = block
            lane = lax.broadcasted_iota(jnp.int32, block.shape, 1)
            vals_ref[pl.ds(pl.multiple_of(spot * BS, BS), BS), :] = jnp.where(
                lane < HD, jnp.ones_like(block), block
            )
            half = per // 2
            qrow = rows + (i % half) * share
            part = got_ref[b, qrow : qrow + share, :]
            if i >= half:
                part = jnp.concatenate([part[:, HD:], part[:, :HD]], axis=1)
            lane = lax.broadcasted_iota(jnp.int32, part.shape, 1)
            q_ref[pl.ds(pl.multiple_of(spot * share, share), share), :] = jnp.where(
                lane < HD, part, jnp.zeros_like(part)
            )
        return carry

    lax.fori_loop(0, sources, place, 0)
    tail = keys_ref.shape[0] - nblocks * BS
    keys_ref[nblocks * BS :, :] = jnp.zeros((tail, 2 * HD), keys_ref.dtype)
    vals_ref[nblocks * BS :, :] = jnp.zeros((tail, 2 * HD), vals_ref.dtype)
    group = GROUP
    wide = WIDE
    tile = group * share

    def score(query, slab):
        return lax.dot_general(
            query, slab, (((1,), (1,)), ((), ())), preferred_element_type=jnp.float32
        )

    def one_image(image, carry):
        count = count_ref[image]
        first = start_ref[image] - count
        text_at = image * TEXT
        shift = text_at % 16
        window = text_ref[pl.ds(pl.multiple_of(text_at - shift, 16), 256), :]
        lane = lax.broadcasted_iota(jnp.int32, window.shape, 1)
        text_vals = jnp.where(lane < HD, jnp.ones_like(window), window)
        spot = lax.broadcasted_iota(jnp.int32, (1, 256), 1)
        text_ok = (spot >= shift) & (spot < shift + TEXT)

        def one_tile(t, carry):
            begin = first + jnp.minimum(t * group, count - group)
            at = pl.multiple_of(begin * share, share)
            query = q_ref[pl.ds(at, tile), :]
            scores = jnp.where(text_ok, score(query, window), neg_large)
            best = jnp.max(scores, axis=1, keepdims=True)
            weights = jnp.exp2((scores - best) * exponent).astype(jnp.bfloat16)
            accum = jnp.dot(weights, text_vals, preferred_element_type=jnp.float32)

            def fold(state, scores, row):
                best, accum = state
                newbest = jnp.maximum(best, jnp.max(scores, axis=1, keepdims=True))
                weights = jnp.exp2((scores - newbest) * exponent).astype(jnp.bfloat16)
                shrink = jnp.exp2((best - newbest) * exponent)
                update = jnp.dot(
                    weights, vals_ref[pl.ds(row, wide * BS), :], preferred_element_type=jnp.float32
                )
                return (newbest, accum * shrink + update)

            def full(c, state):
                row = pl.multiple_of((first + c * wide) * BS, BS)
                return fold(state, score(query, keys_ref[pl.ds(row, wide * BS), :]), row)

            def rest(state):
                done = (count // wide) * wide
                row = pl.multiple_of((first + done) * BS, BS)
                scores = score(query, keys_ref[pl.ds(row, wide * BS), :])
                spot = lax.broadcasted_iota(jnp.int32, (1, wide * BS), 1)
                scores = jnp.where(spot < (count - done) * BS, scores, neg_large)
                return fold(state, scores, row)

            state = lax.fori_loop(0, count // wide, full, (best, accum))
            best, accum = lax.cond(count % wide > 0, rest, lambda state: state, state)
            total = jnp.concatenate([accum[:, HD:], accum[:, :HD]], axis=1)
            o_ref[pl.ds(at, tile), :] = accum / total
            return carry

        return lax.fori_loop(0, (count + group - 1) // group, one_tile, carry)

    lax.fori_loop(0, images, one_image, 0)

    def emit(j, carry):
        at = pl.multiple_of(pos_ref[j] * share, share)
        half = share // 2
        block = o_ref[pl.ds(at, share), :].astype(jnp.bfloat16)
        out_ref[j] = jnp.concatenate([block[:half, HD:], block[half:, HD:]], axis=1)
        return carry

    lax.fori_loop(0, nblocks, emit, 0)


def project_kernel(
    where_ref, image_ref, got_ref, w0_ref, w1_ref, w2_ref, w3_ref, gate_ref, res_ref, out_ref, mixed_ref
):
    groups = mixed_ref.shape[0]
    heads = mixed_ref.shape[2] // HD
    half = got_ref.shape[1]
    parts = got_ref.shape[0] // (groups * heads)
    for g in range(groups):
        for r in range(parts):
            pieces = [got_ref[(h * parts + r) * groups + g] for h in range(heads)]
            low = r * 2 * half
            mixed_ref[g, low : low + half, :] = jnp.concatenate(
                [piece[:, :HD] for piece in pieces], axis=1
            )
            mixed_ref[g, low + half : low + 2 * half, :] = jnp.concatenate(
                [piece[:, HD:] for piece in pieces], axis=1
            )
    me = where_ref[0]
    total = jnp.dot(mixed_ref[me], w0_ref[...], preferred_element_type=jnp.float32)
    for k, w_ref in ((1, w1_ref), (2, w2_ref), (3, w3_ref)):
        total += jnp.dot(mixed_ref[me ^ k], w_ref[...], preferred_element_type=jnp.float32)
    gating = gate_ref[pl.ds(image_ref[where_ref[1]], 1), :]
    out_ref[...] = (res_ref[...].astype(jnp.float32) + gating * total).astype(jnp.bfloat16)


def by_heads(
    queries, key_rows, values, text_keys, text_values, block_image, gate_image, residual, w_out
):
    tok_blk, ncols = queries.shape
    heads = ncols // HD
    nblk = lax.axis_size("blk")
    nhead = lax.axis_size("head")
    nblocks = block_image.shape[0]
    images = gate_image.shape[0]
    parts = nblk // heads
    share = BS // parts
    blk = lax.axis_index("blk")
    head = lax.axis_index("head")
    smem = pl.BlockSpec(memory_space=pltpu.SMEM)
    vmem = pl.BlockSpec(memory_space=pltpu.VMEM)
    packed = tok_blk + tok_blk // parts // 2
    text_rows = round_up(text_keys.shape[0], 16) + 256
    bf16 = jnp.bfloat16
    w1 = lax.ppermute(w_out, "head", [(i, i ^ 1) for i in range(nhead)])
    w2 = lax.ppermute(w_out, "head", [(i, i ^ 2) for i in range(nhead)])
    w3 = lax.ppermute(w2, "head", [(i, i ^ 1) for i in range(nhead)])
    send, text = pl.pallas_call(
        pack_kernel,
        out_shape=(
            jax.ShapeDtypeStruct((nblk, packed, 2 * HD), bf16),
            jax.ShapeDtypeStruct((text_rows, 2 * HD), bf16),
        ),
        in_specs=[smem] + [vmem] * 5,
        out_specs=(vmem, vmem),
        name="pack",
    )((blk // parts).reshape(1), queries, key_rows, values, text_keys, text_values)
    got = lax.all_to_all(send, "blk", split_axis=0, concat_axis=0, tiled=True)
    attended = pl.pallas_call(
        attend_kernel,
        out_shape=jax.ShapeDtypeStruct((nblocks, share // 2, 2 * HD), bf16),
        in_specs=[smem, vmem, vmem],
        out_specs=vmem,
        scratch_shapes=[
            pltpu.VMEM(((nblocks + WIDE) * BS, 2 * HD), bf16),
            pltpu.VMEM(((nblocks + WIDE) * BS, 2 * HD), bf16),
            pltpu.VMEM((nblocks * share, 2 * HD), bf16),
            pltpu.VMEM((nblocks * share, 2 * HD), jnp.float32),
            pltpu.SMEM((images,), jnp.int32),
            pltpu.SMEM((images,), jnp.int32),
            pltpu.SMEM((nblocks,), jnp.int32),
        ],
        cost_estimate=pl.CostEstimate(
            flops=8 * HD * nblocks * nblocks * BS * share,
            transcendentals=nblocks * nblocks * BS * share,
            bytes_accessed=nblk * packed * 4 * HD,
        ),
        name="attend",
    )(block_image, got, text)
    mixed = lax.all_to_all(attended, ("blk", "head"), split_axis=0, concat_axis=0, tiled=True)
    return pl.pallas_call(
        project_kernel,
        out_shape=jax.ShapeDtypeStruct(residual.shape, bf16),
        in_specs=[smem, smem] + [vmem] * 7,
        out_specs=vmem,
        scratch_shapes=[pltpu.VMEM((nhead, BS, ncols), bf16)],
        name="project",
    )(
        jnp.stack([head, blk * nhead + head]),
        block_image,
        mixed,
        w_out,
        w1,
        w2,
        w3,
        gate_image,
        residual,
    )


def solution(mesh):
    placed = (
        P("blk", "head"),
        P("blk", "head"),
        P("blk", "head"),
        P(None, "head"),
        P(None, "head"),
        P(),
        P(),
        P(("blk", "head"), None),
        P("head", None),
    )
    nblk, nhead = mesh.shape["blk"], mesh.shape["head"]

    def step(queries, *others):
        heads = queries.shape[1] // HD
        fits = nhead == 4 and nblk % heads == 0 and nblk // heads in (1, 2, 4)
        fits = fits and queries.shape[0] == nhead * BS
        return (by_heads if fits else on_device)(queries, *others)

    return jax.shard_map(
        step, mesh=mesh, in_specs=placed, out_specs=P(("blk", "head"), None), check_vma=False
    )
```

```python
import math

import jax
import jax.numpy as jnp
from jax import lax
from jax.experimental import pallas as pl
from jax.experimental.pallas import tpu as pltpu
from jax.sharding import PartitionSpec as P

HD = 64
TEXT = 154
BS = 128
GROUP = 2
WIDE = 4


neg_large = -1e30


def absorb(running, query_three, query_image, key_slab, value_slab, key_image):
    best, total, accum = running
    heads = query_three.shape[1]
    width = query_three.shape[2]
    key_three = key_slab.reshape(key_slab.shape[0], heads, width)
    value_three = value_slab.reshape(value_slab.shape[0], heads, width)
    scores = jnp.einsum("qhd,khd->hqk", query_three, key_three, preferred_element_type=jnp.float32)
    scores = scores * (1.0 / math.sqrt(width))
    allowed = query_image[:, None] == key_image[None, :]
    scores = jnp.where(allowed[None], scores, neg_large)
    newbest = jnp.maximum(best, jnp.max(scores, axis=2))
    weights = jnp.exp(scores - newbest[..., None])
    shrink = jnp.exp(best - newbest)
    total = total * shrink + jnp.sum(weights, axis=2)
    update = jnp.einsum(
        "hqk,khd->hqd",
        weights.astype(jnp.bfloat16),
        value_three,
        preferred_element_type=jnp.float32,
    )
    accum = accum * shrink[..., None] + update
    return (newbest, total, accum)


def on_device(
    queries, key_rows, values, text_keys, text_values, block_image, gate_image, residual, w_out
):
    tok_blk = queries.shape[0]
    ncols = queries.shape[1]
    heads_here = ncols // HD
    blocks_here = tok_blk // BS
    token_image = jnp.repeat(block_image, BS)
    blk_index = lax.axis_index("blk")
    my_blocks = lax.dynamic_slice_in_dim(block_image, blk_index * blocks_here, blocks_here)
    query_image = jnp.repeat(my_blocks, BS)
    text_image = jnp.arange(text_keys.shape[0]) // TEXT
    start_state = (
        jnp.full((heads_here, tok_blk), neg_large, jnp.float32),
        jnp.zeros((heads_here, tok_blk), jnp.float32),
        jnp.zeros((heads_here, tok_blk, HD), jnp.float32),
    )
    query_three = queries.reshape(tok_blk, heads_here, HD)
    running = absorb(start_state, query_three, query_image, text_keys, text_values, text_image)
    fold_running = running
    key_piece = lax.all_gather(key_rows, "blk", axis=0, tiled=True)
    value_piece = lax.all_gather(values, "blk", axis=0, tiled=True)
    length = key_piece.shape[0]

    def advance(state, position):
        begin = position * tok_blk
        key_slab = lax.dynamic_slice_in_dim(key_piece, begin, tok_blk)
        value_slab = lax.dynamic_slice_in_dim(value_piece, begin, tok_blk)
        slab_image = lax.dynamic_slice_in_dim(token_image, begin, tok_blk)
        return (absorb(state, query_three, query_image, key_slab, value_slab, slab_image), None)

    fold_running, unused = lax.scan(
        advance, fold_running, jnp.arange(length // tok_blk, dtype=jnp.int32)
    )
    best, total, accum = fold_running
    attended = (accum / total[..., None]).astype(jnp.bfloat16)
    attended = attended.transpose(1, 0, 2).reshape(tok_blk, ncols)
    tok_dev = tok_blk // lax.axis_size("head")
    mixed = lax.all_to_all(attended, "head", split_axis=0, concat_axis=1, tiled=True)
    projected = jnp.dot(
        mixed, lax.all_gather(w_out, "head", axis=0, tiled=True), preferred_element_type=jnp.float32
    )
    head_index = lax.axis_index("head")
    row_image = lax.dynamic_slice_in_dim(query_image, head_index * tok_dev, tok_dev)
    onehot = (
        row_image[:, None] == jnp.arange(gate_image.shape[0], dtype=jnp.int32)[None, :]
    ).astype(jnp.float32)
    gating = jnp.dot(onehot, gate_image, precision=lax.Precision.HIGHEST)
    return (residual.astype(jnp.float32) + gating * projected).astype(jnp.bfloat16)

def round_up(count, unit):
    return -(-count // unit) * unit


def pack_kernel(head_ref, q_ref, k_ref, v_ref, tk_ref, tv_ref, send_ref, text_ref):
    heads = q_ref.shape[1] // HD
    rows = q_ref.shape[0]
    half = rows // 2
    for h in range(heads):
        cols = slice(h * HD, (h + 1) * HD)
        send_ref[h, 0:rows, :] = jnp.concatenate([k_ref[:, cols], v_ref[:, cols]], axis=1)
        send_ref[h, rows : rows + half, :] = jnp.concatenate(
            [q_ref[0:half, cols], q_ref[half:rows, cols]], axis=1
        )
    ntext = tk_ref.shape[0]
    text_ref[...] = jnp.zeros(text_ref.shape, text_ref.dtype)
    for h in range(heads):

        @pl.when(head_ref[0] == h)
        def _():
            cols = slice(h * HD, (h + 1) * HD)
            text_ref[0:ntext, :] = jnp.concatenate([tk_ref[:, cols], tv_ref[:, cols]], axis=1)


EXPONENT = math.log2(math.e) / math.sqrt(HD)


def count_images(image_ref, count_ref, which, parts, sources, per):
    def tally(s, carry):
        for i in range(per):
            image = image_ref[(s * parts + which) * per + i]
            count_ref[image] = count_ref[image] + 1
        return carry

    for i in range(count_ref.shape[0]):
        count_ref[i] = 0
    lax.fori_loop(0, sources, tally, 0)


def put_block(keys_ref, vals_ref, spot, block):
    at = pl.ds(pl.multiple_of(spot * BS, BS), BS)
    lane = lax.broadcasted_iota(jnp.int32, block.shape, 1)
    keys_ref[at, :] = block
    vals_ref[at, :] = jnp.where(lane < HD, jnp.ones_like(block), block)


def score(query, slab):
    return lax.dot_general(query, slab, (((1,), (1,)), ((), ())), preferred_element_type=jnp.float32)


def fold(state, scores, vals):
    best, accum = state
    newbest = jnp.maximum(best, jnp.max(scores, axis=1, keepdims=True))
    weights = jnp.exp2((scores - newbest) * EXPONENT).astype(jnp.bfloat16)
    shrink = jnp.exp2((best - newbest) * EXPONENT)
    update = jnp.dot(weights, vals, preferred_element_type=jnp.float32)
    return (newbest, accum * shrink + update)


def first_kernel(
    image_ref, where_ref, got_ref, text_ref, q_ref, best_ref, accum_ref,
    keys_ref, vals_ref, count_ref, start_ref, qstart_ref
):
    images = count_ref.shape[0]
    sources = got_ref.shape[0]
    rows = got_ref.shape[1] * 2 // 3
    per = rows // BS
    parts = image_ref.shape[0] // (sources * per)
    mine = where_ref[0]
    count_images(image_ref, count_ref, mine, parts, sources, per)
    begin = jnp.int32(0)
    qbegin = jnp.int32(0)
    for i in range(images):
        start_ref[i] = begin
        qstart_ref[i] = qbegin
        begin = begin + count_ref[i]
        qbegin = qbegin + (count_ref[i] + GROUP - 1) // GROUP * GROUP
    q_ref[...] = jnp.zeros(q_ref.shape, q_ref.dtype)

    def place(s, carry):
        for i in range(per):
            image = image_ref[(s * parts + mine) * per + i]
            spot = start_ref[image]
            start_ref[image] = spot + 1
            put_block(keys_ref, vals_ref, spot, got_ref[s, i * BS : (i + 1) * BS, :])
            half = per // 2
            qrow = rows + (i % half) * BS
            part = got_ref[s, qrow : qrow + BS, :]
            if i >= half:
                part = jnp.concatenate([part[:, HD:], part[:, :HD]], axis=1)
            lane = lax.broadcasted_iota(jnp.int32, part.shape, 1)
            qspot = qstart_ref[image]
            qstart_ref[image] = qspot + 1
            q_ref[pl.ds(pl.multiple_of(qspot * BS, BS), BS), :] = jnp.where(
                lane < HD, part, jnp.zeros_like(part)
            )
        return carry

    lax.fori_loop(0, sources, place, 0)

    def one_image(image, carry):
        count = count_ref[image]
        first = start_ref[image] - count
        qfirst = qstart_ref[image] - count
        text_at = image * TEXT
        shift = text_at % 16
        window = text_ref[pl.ds(pl.multiple_of(text_at - shift, 16), 256), :]
        lane = lax.broadcasted_iota(jnp.int32, window.shape, 1)
        text_vals = jnp.where(lane < HD, jnp.ones_like(window), window)
        spot = lax.broadcasted_iota(jnp.int32, (1, 256), 1)
        text_ok = (spot >= shift) & (spot < shift + TEXT)

        def one_tile(t, carry):
            at = pl.ds(pl.multiple_of((qfirst + t * GROUP) * BS, BS), GROUP * BS)
            query = q_ref[at, :]
            scores = jnp.where(text_ok, score(query, window), neg_large)
            best = jnp.max(scores, axis=1, keepdims=True)
            weights = jnp.exp2((scores - best) * EXPONENT).astype(jnp.bfloat16)
            accum = jnp.dot(weights, text_vals, preferred_element_type=jnp.float32)

            def full(c, state):
                row = pl.ds(pl.multiple_of((first + c * WIDE) * BS, BS), WIDE * BS)
                return fold(state, score(query, keys_ref[row, :]), vals_ref[row, :])

            best, accum = lax.fori_loop(0, count // WIDE, full, (best, accum))
            best_ref[at, :] = jnp.broadcast_to(best, accum.shape)
            accum_ref[at, :] = accum
            return carry

        return lax.fori_loop(0, (count + GROUP - 1) // GROUP, one_tile, carry)

    lax.fori_loop(0, images, one_image, 0)


def second_kernel(
    image_ref, where_ref, got_ref, far_ref, q_ref, best_ref, accum_ref, out_ref,
    keys_ref, vals_ref, o_ref, count_ref, start_ref, qstart_ref, far_count_ref, seen_ref, pos_ref
):
    images = count_ref.shape[0]
    sources, rows = far_ref.shape[0], far_ref.shape[1]
    per = rows // BS
    parts = image_ref.shape[0] // (sources * per)
    mine = where_ref[0]
    other = 1 - mine
    count_images(image_ref, count_ref, mine, parts, sources, per)
    count_images(image_ref, far_count_ref, other, parts, sources, per)
    begin = jnp.int32(0)
    qbegin = jnp.int32(0)
    for i in range(images):
        far_count_ref[i] = far_count_ref[i] + count_ref[i] % WIDE
        seen_ref[i] = 0
        start_ref[i] = begin
        qstart_ref[i] = qbegin
        begin = begin + far_count_ref[i]
        qbegin = qbegin + (count_ref[i] + GROUP - 1) // GROUP * GROUP
    keys_ref[...] = jnp.zeros(keys_ref.shape, keys_ref.dtype)
    vals_ref[...] = jnp.zeros(vals_ref.shape, vals_ref.dtype)

    def place(s, carry):
        for i in range(per):
            image = image_ref[(s * parts + other) * per + i]
            spot = start_ref[image]
            start_ref[image] = spot + 1
            put_block(keys_ref, vals_ref, spot, far_ref[s, i * BS : (i + 1) * BS, :])
            image_near = image_ref[(s * parts + mine) * per + i]
            seen = seen_ref[image_near]
            seen_ref[image_near] = seen + 1
            pos_ref[s * per + i] = qstart_ref[image_near] + seen

            @pl.when(seen >= count_ref[image_near] // WIDE * WIDE)
            def _():
                near = start_ref[image_near]
                start_ref[image_near] = near + 1
                put_block(keys_ref, vals_ref, near, got_ref[s, i * BS : (i + 1) * BS, :])

        return carry

    lax.fori_loop(0, sources, place, 0)

    def one_image(image, carry):
        tiles = (count_ref[image] + GROUP - 1) // GROUP
        count = far_count_ref[image]
        first = start_ref[image] - count
        qfirst = qstart_ref[image]

        def one_tile(t, carry):
            at = pl.ds(pl.multiple_of((qfirst + t * GROUP) * BS, BS), GROUP * BS)
            query = q_ref[at, :]

            def full(c, state):
                row = pl.ds(pl.multiple_of((first + c * WIDE) * BS, BS), WIDE * BS)
                return fold(state, score(query, keys_ref[row, :]), vals_ref[row, :])

            def rest(state):
                done = count // WIDE * WIDE
                row = pl.ds(pl.multiple_of((first + done) * BS, BS), WIDE * BS)
                spot = lax.broadcasted_iota(jnp.int32, (1, WIDE * BS), 1)
                scores = score(query, keys_ref[row, :])
                scores = jnp.where(spot < (count - done) * BS, scores, neg_large)
                return fold(state, scores, vals_ref[row, :])

            state = (best_ref[at, :][:, :1], accum_ref[at, :])
            state = lax.fori_loop(0, count // WIDE, full, state)
            best, accum = lax.cond(count % WIDE > 0, rest, lambda state: state, state)
            total = jnp.concatenate([accum[:, HD:], accum[:, :HD]], axis=1)
            o_ref[at, :] = accum / total
            return carry

        return lax.fori_loop(0, tiles, one_tile, carry)

    lax.fori_loop(0, images, one_image, 0)

    def emit(j, carry):
        half = BS // 2
        block = o_ref[pl.ds(pl.multiple_of(pos_ref[j] * BS, BS), BS), :].astype(jnp.bfloat16)
        out_ref[j] = jnp.concatenate([block[:half, HD:], block[half:, HD:]], axis=1)
        return carry

    lax.fori_loop(0, out_ref.shape[0], emit, 0)


def project_kernel(
    where_ref, image_ref, got_ref, w0_ref, w1_ref, w2_ref, w3_ref, gate_ref, res_ref, out_ref, mixed_ref
):
    groups = mixed_ref.shape[0]
    heads = mixed_ref.shape[2] // HD
    half = got_ref.shape[1]
    parts = got_ref.shape[0] // (groups * heads)
    for g in range(groups):
        for r in range(parts):
            pieces = [got_ref[(h * parts + r) * groups + g] for h in range(heads)]
            low = r * 2 * half
            mixed_ref[g, low : low + half, :] = jnp.concatenate(
                [piece[:, :HD] for piece in pieces], axis=1
            )
            mixed_ref[g, low + half : low + 2 * half, :] = jnp.concatenate(
                [piece[:, HD:] for piece in pieces], axis=1
            )
    me = where_ref[0]
    total = jnp.dot(mixed_ref[me], w0_ref[...], preferred_element_type=jnp.float32)
    for k, w_ref in ((1, w1_ref), (2, w2_ref), (3, w3_ref)):
        total += jnp.dot(mixed_ref[me ^ k], w_ref[...], preferred_element_type=jnp.float32)
    gating = gate_ref[pl.ds(image_ref[where_ref[1]], 1), :]
    out_ref[...] = (res_ref[...].astype(jnp.float32) + gating * total).astype(jnp.bfloat16)


def by_heads(
    queries, key_rows, values, text_keys, text_values, block_image, gate_image, residual, w_out
):
    tok_blk, ncols = queries.shape
    heads = ncols // HD
    nblk = lax.axis_size("blk")
    nhead = lax.axis_size("head")
    nblocks = block_image.shape[0]
    images = gate_image.shape[0]
    parts = nblk // heads
    blk = lax.axis_index("blk")
    head = lax.axis_index("head")
    smem = pl.BlockSpec(memory_space=pltpu.SMEM)
    vmem = pl.BlockSpec(memory_space=pltpu.VMEM)
    packed = tok_blk + tok_blk // 2
    local = nblocks // parts
    slots = round_up(local, GROUP) + GROUP * images
    groups = [[s * parts + y for s in range(heads)] for y in range(parts)]
    wide_groups = [[b * nhead + x for b in group for x in range(nhead)] for group in groups]
    text_rows = round_up(text_keys.shape[0], 16) + 256
    bf16 = jnp.bfloat16
    w1 = lax.ppermute(w_out, "head", [(i, i ^ 1) for i in range(nhead)])
    w2 = lax.ppermute(w_out, "head", [(i, i ^ 2) for i in range(nhead)])
    w3 = lax.ppermute(w2, "head", [(i, i ^ 1) for i in range(nhead)])
    send, text = pl.pallas_call(
        pack_kernel,
        out_shape=(
            jax.ShapeDtypeStruct((heads, packed, 2 * HD), bf16),
            jax.ShapeDtypeStruct((text_rows, 2 * HD), bf16),
        ),
        in_specs=[smem] + [vmem] * 5,
        out_specs=(vmem, vmem),
        name="pack",
    )((blk // parts).reshape(1), queries, key_rows, values, text_keys, text_values)
    got = lax.all_to_all(
        send, "blk", split_axis=0, concat_axis=0, tiled=True, axis_index_groups=groups
    )
    swap = [(i, i ^ 1) for i in range(nblk)]
    far = lax.ppermute(got[:, :tok_blk], "blk", swap)
    mine = (blk % parts).reshape(1)
    state_shape = (slots * BS, 2 * HD)
    state = pl.pallas_call(
        first_kernel,
        out_shape=(
            jax.ShapeDtypeStruct(state_shape, bf16),
            jax.ShapeDtypeStruct(state_shape, jnp.float32),
            jax.ShapeDtypeStruct(state_shape, jnp.float32),
        ),
        in_specs=[smem, smem, vmem, vmem],
        out_specs=(vmem, vmem, vmem),
        scratch_shapes=[pltpu.VMEM((local * BS, 2 * HD), bf16)] * 2
        + [pltpu.SMEM((images,), jnp.int32)] * 3,
        cost_estimate=pl.CostEstimate(
            flops=8 * HD * local * local * BS * BS,
            transcendentals=local * local * BS * BS,
            bytes_accessed=heads * packed * 4 * HD,
        ),
        name="attend_near",
    )(block_image, mine, got, text)
    key_slots = local + (WIDE - 1) * images + WIDE
    attended = pl.pallas_call(
        second_kernel,
        out_shape=jax.ShapeDtypeStruct((local, BS // 2, 2 * HD), bf16),
        in_specs=[smem, smem] + [vmem] * 5,
        out_specs=vmem,
        scratch_shapes=[pltpu.VMEM((key_slots * BS, 2 * HD), bf16)] * 2
        + [pltpu.VMEM(state_shape, jnp.float32)]
        + [pltpu.SMEM((images,), jnp.int32)] * 5
        + [pltpu.SMEM((local,), jnp.int32)],
        cost_estimate=pl.CostEstimate(
            flops=8 * HD * local * local * BS * BS,
            transcendentals=local * local * BS * BS,
            bytes_accessed=heads * packed * 4 * HD,
        ),
        name="attend_far",
    )(block_image, mine, got, far, *state)
    mixed = lax.all_to_all(
        attended,
        ("blk", "head"),
        split_axis=0,
        concat_axis=0,
        tiled=True,
        axis_index_groups=wide_groups,
    )
    return pl.pallas_call(
        project_kernel,
        out_shape=jax.ShapeDtypeStruct(residual.shape, bf16),
        in_specs=[smem, smem] + [vmem] * 7,
        out_specs=vmem,
        scratch_shapes=[pltpu.VMEM((nhead, BS, ncols), bf16)],
        name="project",
    )(
        jnp.stack([head, blk * nhead + head]),
        block_image,
        mixed,
        w_out,
        w1,
        w2,
        w3,
        gate_image,
        residual,
    )


def solution(mesh):
    placed = (
        P("blk", "head"),
        P("blk", "head"),
        P("blk", "head"),
        P(None, "head"),
        P(None, "head"),
        P(),
        P(),
        P(("blk", "head"), None),
        P("head", None),
    )
    nblk, nhead = mesh.shape["blk"], mesh.shape["head"]

    def step(queries, *others):
        heads = queries.shape[1] // HD
        fits = nhead == 4 and nblk % heads == 0 and nblk == 2 * heads
        fits = fits and queries.shape[0] == nhead * BS
        return (by_heads if fits else on_device)(queries, *others)

    return jax.shard_map(
        step, mesh=mesh, in_specs=placed, out_specs=P(("blk", "head"), None), check_vma=False
    )
```

```python
import math

import jax
import jax.numpy as jnp
from jax import lax
from jax.experimental import pallas as pl
from jax.experimental.pallas import tpu as pltpu
from jax.sharding import PartitionSpec as P

HD = 64
TEXT = 154
BS = 128
GROUP = 2
WIDE = 8


neg_large = -1e30


def absorb(running, query_three, query_image, key_slab, value_slab, key_image):
    best, total, accum = running
    heads = query_three.shape[1]
    width = query_three.shape[2]
    key_three = key_slab.reshape(key_slab.shape[0], heads, width)
    value_three = value_slab.reshape(value_slab.shape[0], heads, width)
    scores = jnp.einsum("qhd,khd->hqk", query_three, key_three, preferred_element_type=jnp.float32)
    scores = scores * (1.0 / math.sqrt(width))
    allowed = query_image[:, None] == key_image[None, :]
    scores = jnp.where(allowed[None], scores, neg_large)
    newbest = jnp.maximum(best, jnp.max(scores, axis=2))
    weights = jnp.exp(scores - newbest[..., None])
    shrink = jnp.exp(best - newbest)
    total = total * shrink + jnp.sum(weights, axis=2)
    update = jnp.einsum(
        "hqk,khd->hqd",
        weights.astype(jnp.bfloat16),
        value_three,
        preferred_element_type=jnp.float32,
    )
    accum = accum * shrink[..., None] + update
    return (newbest, total, accum)


def on_device(
    queries, key_rows, values, text_keys, text_values, block_image, gate_image, residual, w_out
):
    tok_blk = queries.shape[0]
    ncols = queries.shape[1]
    heads_here = ncols // HD
    blocks_here = tok_blk // BS
    token_image = jnp.repeat(block_image, BS)
    blk_index = lax.axis_index("blk")
    my_blocks = lax.dynamic_slice_in_dim(block_image, blk_index * blocks_here, blocks_here)
    query_image = jnp.repeat(my_blocks, BS)
    text_image = jnp.arange(text_keys.shape[0]) // TEXT
    start_state = (
        jnp.full((heads_here, tok_blk), neg_large, jnp.float32),
        jnp.zeros((heads_here, tok_blk), jnp.float32),
        jnp.zeros((heads_here, tok_blk, HD), jnp.float32),
    )
    query_three = queries.reshape(tok_blk, heads_here, HD)
    running = absorb(start_state, query_three, query_image, text_keys, text_values, text_image)
    fold_running = running
    key_piece = lax.all_gather(key_rows, "blk", axis=0, tiled=True)
    value_piece = lax.all_gather(values, "blk", axis=0, tiled=True)
    length = key_piece.shape[0]

    def advance(state, position):
        begin = position * tok_blk
        key_slab = lax.dynamic_slice_in_dim(key_piece, begin, tok_blk)
        value_slab = lax.dynamic_slice_in_dim(value_piece, begin, tok_blk)
        slab_image = lax.dynamic_slice_in_dim(token_image, begin, tok_blk)
        return (absorb(state, query_three, query_image, key_slab, value_slab, slab_image), None)

    fold_running, unused = lax.scan(
        advance, fold_running, jnp.arange(length // tok_blk, dtype=jnp.int32)
    )
    best, total, accum = fold_running
    attended = (accum / total[..., None]).astype(jnp.bfloat16)
    attended = attended.transpose(1, 0, 2).reshape(tok_blk, ncols)
    tok_dev = tok_blk // lax.axis_size("head")
    mixed = lax.all_to_all(attended, "head", split_axis=0, concat_axis=1, tiled=True)
    projected = jnp.dot(
        mixed, lax.all_gather(w_out, "head", axis=0, tiled=True), preferred_element_type=jnp.float32
    )
    head_index = lax.axis_index("head")
    row_image = lax.dynamic_slice_in_dim(query_image, head_index * tok_dev, tok_dev)
    onehot = (
        row_image[:, None] == jnp.arange(gate_image.shape[0], dtype=jnp.int32)[None, :]
    ).astype(jnp.float32)
    gating = jnp.dot(onehot, gate_image, precision=lax.Precision.HIGHEST)
    return (residual.astype(jnp.float32) + gating * projected).astype(jnp.bfloat16)

def round_up(count, unit):
    return -(-count // unit) * unit


def pack_kernel(head_ref, q_ref, k_ref, v_ref, tk_ref, tv_ref, send_ref, text_ref):
    heads = q_ref.shape[1] // HD
    rows = q_ref.shape[0]
    half = rows // 2
    for h in range(heads):
        cols = slice(h * HD, (h + 1) * HD)
        send_ref[h, 0:rows, :] = jnp.concatenate([k_ref[:, cols], v_ref[:, cols]], axis=1)
        send_ref[h, rows : rows + half, :] = jnp.concatenate(
            [q_ref[0:half, cols], q_ref[half:rows, cols]], axis=1
        )
    ntext = tk_ref.shape[0]
    text_ref[...] = jnp.zeros(text_ref.shape, text_ref.dtype)
    for h in range(heads):

        @pl.when(head_ref[0] == h)
        def _():
            cols = slice(h * HD, (h + 1) * HD)
            text_ref[0:ntext, :] = jnp.concatenate([tk_ref[:, cols], tv_ref[:, cols]], axis=1)


EXPONENT = math.log2(math.e) / math.sqrt(HD)


def count_images(image_ref, count_ref, which, parts, sources, per):
    def tally(s, carry):
        for i in range(per):
            image = image_ref[(s * parts + which) * per + i]
            count_ref[image] = count_ref[image] + 1
        return carry

    for i in range(count_ref.shape[0]):
        count_ref[i] = 0
    lax.fori_loop(0, sources, tally, 0)


def put_block(keys_ref, vals_ref, spot, block):
    at = pl.ds(pl.multiple_of(spot * BS, BS), BS)
    lane = lax.broadcasted_iota(jnp.int32, block.shape, 1)
    keys_ref[at, :] = block
    vals_ref[at, :] = jnp.where(lane < HD, jnp.ones_like(block), block)


def score(query, slab):
    return lax.dot_general(query, slab, (((1,), (1,)), ((), ())), preferred_element_type=jnp.float32)


def fold(state, scores, vals):
    best, accum = state
    newbest = jnp.maximum(best, jnp.max(scores, axis=1, keepdims=True))
    weights = jnp.exp2((scores - newbest) * EXPONENT).astype(jnp.bfloat16)
    shrink = jnp.exp2((best - newbest) * EXPONENT)
    update = jnp.dot(weights, vals, preferred_element_type=jnp.float32)
    return (newbest, accum * shrink + update)


def first_kernel(
    image_ref, where_ref, got_ref, text_ref, q_ref, best_ref, accum_ref,
    keys_ref, vals_ref, count_ref, start_ref, qstart_ref
):
    images = count_ref.shape[0]
    sources = got_ref.shape[0]
    rows = got_ref.shape[1] * 2 // 3
    per = rows // BS
    parts = image_ref.shape[0] // (sources * per)
    mine = where_ref[0]
    count_images(image_ref, count_ref, mine, parts, sources, per)
    begin = jnp.int32(0)
    qbegin = jnp.int32(0)
    for i in range(images):
        start_ref[i] = begin
        qstart_ref[i] = qbegin
        begin = begin + count_ref[i]
        qbegin = qbegin + (count_ref[i] + GROUP - 1) // GROUP * GROUP
    q_ref[...] = jnp.zeros(q_ref.shape, q_ref.dtype)

    def place(s, carry):
        for i in range(per):
            image = image_ref[(s * parts + mine) * per + i]
            spot = start_ref[image]
            start_ref[image] = spot + 1
            put_block(keys_ref, vals_ref, spot, got_ref[s, i * BS : (i + 1) * BS, :])
            half = per // 2
            qrow = rows + (i % half) * BS
            part = got_ref[s, qrow : qrow + BS, :]
            if i >= half:
                part = jnp.concatenate([part[:, HD:], part[:, :HD]], axis=1)
            lane = lax.broadcasted_iota(jnp.int32, part.shape, 1)
            qspot = qstart_ref[image]
            qstart_ref[image] = qspot + 1
            q_ref[pl.ds(pl.multiple_of(qspot * BS, BS), BS), :] = jnp.where(
                lane < HD, part, jnp.zeros_like(part)
            )
        return carry

    lax.fori_loop(0, sources, place, 0)

    def one_image(image, carry):
        count = count_ref[image]
        first = start_ref[image] - count
        qfirst = qstart_ref[image] - count
        text_at = image * TEXT
        shift = text_at % 16
        window = text_ref[pl.ds(pl.multiple_of(text_at - shift, 16), 256), :]
        lane = lax.broadcasted_iota(jnp.int32, window.shape, 1)
        text_vals = jnp.where(lane < HD, jnp.ones_like(window), window)
        spot = lax.broadcasted_iota(jnp.int32, (1, 256), 1)
        text_ok = (spot >= shift) & (spot < shift + TEXT)

        def one_tile(t, carry):
            at = pl.ds(pl.multiple_of((qfirst + t * GROUP) * BS, BS), GROUP * BS)
            query = q_ref[at, :]
            scores = jnp.where(text_ok, score(query, window), neg_large)
            best = jnp.max(scores, axis=1, keepdims=True)
            weights = jnp.exp2((scores - best) * EXPONENT).astype(jnp.bfloat16)
            accum = jnp.dot(weights, text_vals, preferred_element_type=jnp.float32)

            def full(c, state):
                row = pl.ds(pl.multiple_of((first + c * WIDE) * BS, BS), WIDE * BS)
                return fold(state, score(query, keys_ref[row, :]), vals_ref[row, :])

            best, accum = lax.fori_loop(0, count // WIDE, full, (best, accum))
            best_ref[at, :] = jnp.broadcast_to(best, accum.shape)
            accum_ref[at, :] = accum
            return carry

        return lax.fori_loop(0, (count + GROUP - 1) // GROUP, one_tile, carry)

    lax.fori_loop(0, images, one_image, 0)


def second_kernel(
    image_ref, where_ref, got_ref, far_ref, q_ref, best_ref, accum_ref, out_ref,
    keys_ref, vals_ref, o_ref, count_ref, start_ref, qstart_ref, far_count_ref, seen_ref, pos_ref
):
    images = count_ref.shape[0]
    sources, rows = far_ref.shape[0], far_ref.shape[1]
    per = rows // BS
    parts = image_ref.shape[0] // (sources * per)
    mine = where_ref[0]
    other = 1 - mine
    count_images(image_ref, count_ref, mine, parts, sources, per)
    count_images(image_ref, far_count_ref, other, parts, sources, per)
    begin = jnp.int32(0)
    qbegin = jnp.int32(0)
    for i in range(images):
        far_count_ref[i] = far_count_ref[i] + count_ref[i] % WIDE
        seen_ref[i] = 0
        start_ref[i] = begin
        qstart_ref[i] = qbegin
        begin = begin + far_count_ref[i]
        qbegin = qbegin + (count_ref[i] + GROUP - 1) // GROUP * GROUP
    keys_ref[...] = jnp.zeros(keys_ref.shape, keys_ref.dtype)
    vals_ref[...] = jnp.zeros(vals_ref.shape, vals_ref.dtype)

    def place(s, carry):
        for i in range(per):
            image = image_ref[(s * parts + other) * per + i]
            spot = start_ref[image]
            start_ref[image] = spot + 1
            put_block(keys_ref, vals_ref, spot, far_ref[s, i * BS : (i + 1) * BS, :])
            image_near = image_ref[(s * parts + mine) * per + i]
            seen = seen_ref[image_near]
            seen_ref[image_near] = seen + 1
            pos_ref[s * per + i] = qstart_ref[image_near] + seen

            @pl.when(seen >= count_ref[image_near] // WIDE * WIDE)
            def _():
                near = start_ref[image_near]
                start_ref[image_near] = near + 1
                put_block(keys_ref, vals_ref, near, got_ref[s, i * BS : (i + 1) * BS, :])

        return carry

    lax.fori_loop(0, sources, place, 0)

    def one_image(image, carry):
        tiles = (count_ref[image] + GROUP - 1) // GROUP
        count = far_count_ref[image]
        first = start_ref[image] - count
        qfirst = qstart_ref[image]

        def one_tile(t, carry):
            at = pl.ds(pl.multiple_of((qfirst + t * GROUP) * BS, BS), GROUP * BS)
            query = q_ref[at, :]

            def full(c, state):
                row = pl.ds(pl.multiple_of((first + c * WIDE) * BS, BS), WIDE * BS)
                return fold(state, score(query, keys_ref[row, :]), vals_ref[row, :])

            def rest(state):
                done = count // WIDE * WIDE
                row = pl.ds(pl.multiple_of((first + done) * BS, BS), WIDE * BS)
                spot = lax.broadcasted_iota(jnp.int32, (1, WIDE * BS), 1)
                scores = score(query, keys_ref[row, :])
                scores = jnp.where(spot < (count - done) * BS, scores, neg_large)
                return fold(state, scores, vals_ref[row, :])

            state = (best_ref[at, :][:, :1], accum_ref[at, :])
            state = lax.fori_loop(0, count // WIDE, full, state)
            best, accum = lax.cond(count % WIDE > 0, rest, lambda state: state, state)
            total = jnp.concatenate([accum[:, HD:], accum[:, :HD]], axis=1)
            o_ref[at, :] = accum / total
            return carry

        return lax.fori_loop(0, tiles, one_tile, carry)

    lax.fori_loop(0, images, one_image, 0)

    def emit(j, carry):
        half = BS // 2
        block = o_ref[pl.ds(pl.multiple_of(pos_ref[j] * BS, BS), BS), :].astype(jnp.bfloat16)
        out_ref[j] = jnp.concatenate([block[:half, HD:], block[half:, HD:]], axis=1)
        return carry

    lax.fori_loop(0, out_ref.shape[0], emit, 0)


def project_kernel(
    where_ref, image_ref, got_ref, w0_ref, w1_ref, w2_ref, w3_ref, gate_ref, res_ref, out_ref, mixed_ref
):
    groups = mixed_ref.shape[0]
    heads = mixed_ref.shape[2] // HD
    half = got_ref.shape[1]
    parts = got_ref.shape[0] // (groups * heads)
    for g in range(groups):
        for r in range(parts):
            pieces = [got_ref[(h * parts + r) * groups + g] for h in range(heads)]
            low = r * 2 * half
            mixed_ref[g, low : low + half, :] = jnp.concatenate(
                [piece[:, :HD] for piece in pieces], axis=1
            )
            mixed_ref[g, low + half : low + 2 * half, :] = jnp.concatenate(
                [piece[:, HD:] for piece in pieces], axis=1
            )
    me = where_ref[0]
    total = jnp.dot(mixed_ref[me], w0_ref[...], preferred_element_type=jnp.float32)
    for k, w_ref in ((1, w1_ref), (2, w2_ref), (3, w3_ref)):
        total += jnp.dot(mixed_ref[me ^ k], w_ref[...], preferred_element_type=jnp.float32)
    gating = gate_ref[pl.ds(image_ref[where_ref[1]], 1), :]
    out_ref[...] = (res_ref[...].astype(jnp.float32) + gating * total).astype(jnp.bfloat16)


def by_heads(
    queries, key_rows, values, text_keys, text_values, block_image, gate_image, residual, w_out
):
    tok_blk, ncols = queries.shape
    heads = ncols // HD
    nblk = lax.axis_size("blk")
    nhead = lax.axis_size("head")
    nblocks = block_image.shape[0]
    images = gate_image.shape[0]
    parts = nblk // heads
    blk = lax.axis_index("blk")
    head = lax.axis_index("head")
    smem = pl.BlockSpec(memory_space=pltpu.SMEM)
    vmem = pl.BlockSpec(memory_space=pltpu.VMEM)
    packed = tok_blk + tok_blk // 2
    local = nblocks // parts
    slots = round_up(local, GROUP) + GROUP * images
    groups = [[s * parts + y for s in range(heads)] for y in range(parts)]
    wide_groups = [[b * nhead + x for b in group for x in range(nhead)] for group in groups]
    text_rows = round_up(text_keys.shape[0], 16) + 256
    bf16 = jnp.bfloat16
    w1 = lax.ppermute(w_out, "head", [(i, i ^ 1) for i in range(nhead)])
    w2 = lax.ppermute(w_out, "head", [(i, i ^ 2) for i in range(nhead)])
    w3 = lax.ppermute(w2, "head", [(i, i ^ 1) for i in range(nhead)])
    send, text = pl.pallas_call(
        pack_kernel,
        out_shape=(
            jax.ShapeDtypeStruct((heads, packed, 2 * HD), bf16),
            jax.ShapeDtypeStruct((text_rows, 2 * HD), bf16),
        ),
        in_specs=[smem] + [vmem] * 5,
        out_specs=(vmem, vmem),
        name="pack",
    )((blk // parts).reshape(1), queries, key_rows, values, text_keys, text_values)
    got = lax.all_to_all(
        send, "blk", split_axis=0, concat_axis=0, tiled=True, axis_index_groups=groups
    )
    swap = [(i, i ^ 1) for i in range(nblk)]
    far = lax.ppermute(got[:, :tok_blk], "blk", swap)
    mine = (blk % parts).reshape(1)
    state_shape = (slots * BS, 2 * HD)
    state = pl.pallas_call(
        first_kernel,
        out_shape=(
            jax.ShapeDtypeStruct(state_shape, bf16),
            jax.ShapeDtypeStruct(state_shape, jnp.float32),
            jax.ShapeDtypeStruct(state_shape, jnp.float32),
        ),
        in_specs=[smem, smem, vmem, vmem],
        out_specs=(vmem, vmem, vmem),
        scratch_shapes=[pltpu.VMEM((local * BS, 2 * HD), bf16)] * 2
        + [pltpu.SMEM((images,), jnp.int32)] * 3,
        cost_estimate=pl.CostEstimate(
            flops=8 * HD * local * local * BS * BS,
            transcendentals=local * local * BS * BS,
            bytes_accessed=heads * packed * 4 * HD,
        ),
        name="attend_near",
    )(block_image, mine, got, text)
    key_slots = local + (WIDE - 1) * images + WIDE
    attended = pl.pallas_call(
        second_kernel,
        out_shape=jax.ShapeDtypeStruct((local, BS // 2, 2 * HD), bf16),
        in_specs=[smem, smem] + [vmem] * 5,
        out_specs=vmem,
        scratch_shapes=[pltpu.VMEM((key_slots * BS, 2 * HD), bf16)] * 2
        + [pltpu.VMEM(state_shape, jnp.float32)]
        + [pltpu.SMEM((images,), jnp.int32)] * 5
        + [pltpu.SMEM((local,), jnp.int32)],
        cost_estimate=pl.CostEstimate(
            flops=8 * HD * local * local * BS * BS,
            transcendentals=local * local * BS * BS,
            bytes_accessed=heads * packed * 4 * HD,
        ),
        name="attend_far",
    )(block_image, mine, got, far, *state)
    mixed = lax.all_to_all(
        attended,
        ("blk", "head"),
        split_axis=0,
        concat_axis=0,
        tiled=True,
        axis_index_groups=wide_groups,
    )
    return pl.pallas_call(
        project_kernel,
        out_shape=jax.ShapeDtypeStruct(residual.shape, bf16),
        in_specs=[smem, smem] + [vmem] * 7,
        out_specs=vmem,
        scratch_shapes=[pltpu.VMEM((nhead, BS, ncols), bf16)],
        name="project",
    )(
        jnp.stack([head, blk * nhead + head]),
        block_image,
        mixed,
        w_out,
        w1,
        w2,
        w3,
        gate_image,
        residual,
    )


def solution(mesh):
    placed = (
        P("blk", "head"),
        P("blk", "head"),
        P("blk", "head"),
        P(None, "head"),
        P(None, "head"),
        P(),
        P(),
        P(("blk", "head"), None),
        P("head", None),
    )
    nblk, nhead = mesh.shape["blk"], mesh.shape["head"]

    def step(queries, *others):
        heads = queries.shape[1] // HD
        fits = nhead == 4 and nblk % heads == 0 and nblk == 2 * heads
        fits = fits and queries.shape[0] == nhead * BS
        return (by_heads if fits else on_device)(queries, *others)

    return jax.shard_map(
        step, mesh=mesh, in_specs=placed, out_specs=P(("blk", "head"), None), check_vma=False
    )
```

```python
import math

import jax
import jax.numpy as jnp
from jax import lax
from jax.experimental import pallas as pl
from jax.experimental.pallas import tpu as pltpu
from jax.sharding import PartitionSpec as P

HD = 64
TEXT = 154
BS = 128
GROUP = 4
WIDE = 8


neg_large = -1e30


def absorb(running, query_three, query_image, key_slab, value_slab, key_image):
    best, total, accum = running
    heads = query_three.shape[1]
    width = query_three.shape[2]
    key_three = key_slab.reshape(key_slab.shape[0], heads, width)
    value_three = value_slab.reshape(value_slab.shape[0], heads, width)
    scores = jnp.einsum("qhd,khd->hqk", query_three, key_three, preferred_element_type=jnp.float32)
    scores = scores * (1.0 / math.sqrt(width))
    allowed = query_image[:, None] == key_image[None, :]
    scores = jnp.where(allowed[None], scores, neg_large)
    newbest = jnp.maximum(best, jnp.max(scores, axis=2))
    weights = jnp.exp(scores - newbest[..., None])
    shrink = jnp.exp(best - newbest)
    total = total * shrink + jnp.sum(weights, axis=2)
    update = jnp.einsum(
        "hqk,khd->hqd",
        weights.astype(jnp.bfloat16),
        value_three,
        preferred_element_type=jnp.float32,
    )
    accum = accum * shrink[..., None] + update
    return (newbest, total, accum)


def on_device(
    queries, key_rows, values, text_keys, text_values, block_image, gate_image, residual, w_out
):
    tok_blk = queries.shape[0]
    ncols = queries.shape[1]
    heads_here = ncols // HD
    blocks_here = tok_blk // BS
    token_image = jnp.repeat(block_image, BS)
    blk_index = lax.axis_index("blk")
    my_blocks = lax.dynamic_slice_in_dim(block_image, blk_index * blocks_here, blocks_here)
    query_image = jnp.repeat(my_blocks, BS)
    text_image = jnp.arange(text_keys.shape[0]) // TEXT
    start_state = (
        jnp.full((heads_here, tok_blk), neg_large, jnp.float32),
        jnp.zeros((heads_here, tok_blk), jnp.float32),
        jnp.zeros((heads_here, tok_blk, HD), jnp.float32),
    )
    query_three = queries.reshape(tok_blk, heads_here, HD)
    running = absorb(start_state, query_three, query_image, text_keys, text_values, text_image)
    fold_running = running
    key_piece = lax.all_gather(key_rows, "blk", axis=0, tiled=True)
    value_piece = lax.all_gather(values, "blk", axis=0, tiled=True)
    length = key_piece.shape[0]

    def advance(state, position):
        begin = position * tok_blk
        key_slab = lax.dynamic_slice_in_dim(key_piece, begin, tok_blk)
        value_slab = lax.dynamic_slice_in_dim(value_piece, begin, tok_blk)
        slab_image = lax.dynamic_slice_in_dim(token_image, begin, tok_blk)
        return (absorb(state, query_three, query_image, key_slab, value_slab, slab_image), None)

    fold_running, unused = lax.scan(
        advance, fold_running, jnp.arange(length // tok_blk, dtype=jnp.int32)
    )
    best, total, accum = fold_running
    attended = (accum / total[..., None]).astype(jnp.bfloat16)
    attended = attended.transpose(1, 0, 2).reshape(tok_blk, ncols)
    tok_dev = tok_blk // lax.axis_size("head")
    mixed = lax.all_to_all(attended, "head", split_axis=0, concat_axis=1, tiled=True)
    projected = jnp.dot(
        mixed, lax.all_gather(w_out, "head", axis=0, tiled=True), preferred_element_type=jnp.float32
    )
    head_index = lax.axis_index("head")
    row_image = lax.dynamic_slice_in_dim(query_image, head_index * tok_dev, tok_dev)
    onehot = (
        row_image[:, None] == jnp.arange(gate_image.shape[0], dtype=jnp.int32)[None, :]
    ).astype(jnp.float32)
    gating = jnp.dot(onehot, gate_image, precision=lax.Precision.HIGHEST)
    return (residual.astype(jnp.float32) + gating * projected).astype(jnp.bfloat16)

def round_up(count, unit):
    return -(-count // unit) * unit


def pack_kernel(head_ref, q_ref, k_ref, v_ref, tk_ref, tv_ref, send_ref, text_ref):
    heads = q_ref.shape[1] // HD
    rows = q_ref.shape[0]
    half = rows // 2
    for h in range(heads):
        cols = slice(h * HD, (h + 1) * HD)
        send_ref[h, 0:rows, :] = jnp.concatenate([k_ref[:, cols], v_ref[:, cols]], axis=1)
        send_ref[h, rows : rows + half, :] = jnp.concatenate(
            [q_ref[0:half, cols], q_ref[half:rows, cols]], axis=1
        )
    ntext = tk_ref.shape[0]
    text_ref[...] = jnp.zeros(text_ref.shape, text_ref.dtype)
    for h in range(heads):

        @pl.when(head_ref[0] == h)
        def _():
            cols = slice(h * HD, (h + 1) * HD)
            text_ref[0:ntext, :] = jnp.concatenate([tk_ref[:, cols], tv_ref[:, cols]], axis=1)


EXPONENT = math.log2(math.e) / math.sqrt(HD)


def count_images(image_ref, count_ref, which, parts, sources, per):
    def tally(s, carry):
        for i in range(per):
            image = image_ref[(s * parts + which) * per + i]
            count_ref[image] = count_ref[image] + 1
        return carry

    for i in range(count_ref.shape[0]):
        count_ref[i] = 0
    lax.fori_loop(0, sources, tally, 0)


def put_block(keys_ref, vals_ref, spot, block):
    at = pl.ds(pl.multiple_of(spot * BS, BS), BS)
    lane = lax.broadcasted_iota(jnp.int32, block.shape, 1)
    keys_ref[at, :] = block
    vals_ref[at, :] = jnp.where(lane < HD, jnp.ones_like(block), block)


def score(query, slab):
    return lax.dot_general(query, slab, (((1,), (1,)), ((), ())), preferred_element_type=jnp.float32)


def fold(state, scores, vals):
    best, accum = state
    newbest = jnp.maximum(best, jnp.max(scores, axis=1, keepdims=True))
    weights = jnp.exp2((scores - newbest) * EXPONENT).astype(jnp.bfloat16)
    shrink = jnp.exp2((best - newbest) * EXPONENT)
    update = jnp.dot(weights, vals, preferred_element_type=jnp.float32)
    return (newbest, accum * shrink + update)


def first_kernel(
    image_ref, where_ref, got_ref, text_ref, q_ref, best_ref, accum_ref,
    keys_ref, vals_ref, count_ref, start_ref, qstart_ref
):
    images = count_ref.shape[0]
    sources = got_ref.shape[0]
    rows = got_ref.shape[1] * 2 // 3
    per = rows // BS
    parts = image_ref.shape[0] // (sources * per)
    mine = where_ref[0]
    count_images(image_ref, count_ref, mine, parts, sources, per)
    begin = jnp.int32(0)
    qbegin = jnp.int32(0)
    for i in range(images):
        start_ref[i] = begin
        qstart_ref[i] = qbegin
        begin = begin + count_ref[i]
        qbegin = qbegin + (count_ref[i] + GROUP - 1) // GROUP * GROUP
    q_ref[...] = jnp.zeros(q_ref.shape, q_ref.dtype)

    def place(s, carry):
        for i in range(per):
            image = image_ref[(s * parts + mine) * per + i]
            spot = start_ref[image]
            start_ref[image] = spot + 1
            put_block(keys_ref, vals_ref, spot, got_ref[s, i * BS : (i + 1) * BS, :])
            half = per // 2
            qrow = rows + (i % half) * BS
            part = got_ref[s, qrow : qrow + BS, :]
            if i >= half:
                part = jnp.concatenate([part[:, HD:], part[:, :HD]], axis=1)
            lane = lax.broadcasted_iota(jnp.int32, part.shape, 1)
            qspot = qstart_ref[image]
            qstart_ref[image] = qspot + 1
            q_ref[pl.ds(pl.multiple_of(qspot * BS, BS), BS), :] = jnp.where(
                lane < HD, part, jnp.zeros_like(part)
            )
        return carry

    lax.fori_loop(0, sources, place, 0)

    def one_image(image, carry):
        count = count_ref[image]
        first = start_ref[image] - count
        qfirst = qstart_ref[image] - count
        text_at = image * TEXT
        shift = text_at % 16
        window = text_ref[pl.ds(pl.multiple_of(text_at - shift, 16), 256), :]
        lane = lax.broadcasted_iota(jnp.int32, window.shape, 1)
        text_vals = jnp.where(lane < HD, jnp.ones_like(window), window)
        spot = lax.broadcasted_iota(jnp.int32, (1, 256), 1)
        text_ok = (spot >= shift) & (spot < shift + TEXT)

        def one_tile(t, carry):
            at = pl.ds(pl.multiple_of((qfirst + t * GROUP) * BS, BS), GROUP * BS)
            query = q_ref[at, :]
            scores = jnp.where(text_ok, score(query, window), neg_large)
            best = jnp.max(scores, axis=1, keepdims=True)
            weights = jnp.exp2((scores - best) * EXPONENT).astype(jnp.bfloat16)
            accum = jnp.dot(weights, text_vals, preferred_element_type=jnp.float32)

            def full(c, state):
                row = pl.ds(pl.multiple_of((first + c * WIDE) * BS, BS), WIDE * BS)
                return fold(state, score(query, keys_ref[row, :]), vals_ref[row, :])

            best, accum = lax.fori_loop(0, count // WIDE, full, (best, accum))
            best_ref[at, :] = jnp.broadcast_to(best, accum.shape)
            accum_ref[at, :] = accum
            return carry

        return lax.fori_loop(0, (count + GROUP - 1) // GROUP, one_tile, carry)

    lax.fori_loop(0, images, one_image, 0)


def second_kernel(
    image_ref, where_ref, got_ref, far_ref, q_ref, best_ref, accum_ref, out_ref,
    keys_ref, vals_ref, o_ref, count_ref, start_ref, qstart_ref, far_count_ref, seen_ref, pos_ref
):
    images = count_ref.shape[0]
    sources, rows = far_ref.shape[0], far_ref.shape[1]
    per = rows // BS
    parts = image_ref.shape[0] // (sources * per)
    mine = where_ref[0]
    other = 1 - mine
    count_images(image_ref, count_ref, mine, parts, sources, per)
    count_images(image_ref, far_count_ref, other, parts, sources, per)
    begin = jnp.int32(0)
    qbegin = jnp.int32(0)
    for i in range(images):
        far_count_ref[i] = far_count_ref[i] + count_ref[i] % WIDE
        seen_ref[i] = 0
        start_ref[i] = begin
        qstart_ref[i] = qbegin
        begin = begin + far_count_ref[i]
        qbegin = qbegin + (count_ref[i] + GROUP - 1) // GROUP * GROUP
    keys_ref[...] = jnp.zeros(keys_ref.shape, keys_ref.dtype)
    vals_ref[...] = jnp.zeros(vals_ref.shape, vals_ref.dtype)

    def place(s, carry):
        for i in range(per):
            image = image_ref[(s * parts + other) * per + i]
            spot = start_ref[image]
            start_ref[image] = spot + 1
            put_block(keys_ref, vals_ref, spot, far_ref[s, i * BS : (i + 1) * BS, :])
            image_near = image_ref[(s * parts + mine) * per + i]
            seen = seen_ref[image_near]
            seen_ref[image_near] = seen + 1
            pos_ref[s * per + i] = qstart_ref[image_near] + seen

            @pl.when(seen >= count_ref[image_near] // WIDE * WIDE)
            def _():
                near = start_ref[image_near]
                start_ref[image_near] = near + 1
                put_block(keys_ref, vals_ref, near, got_ref[s, i * BS : (i + 1) * BS, :])

        return carry

    lax.fori_loop(0, sources, place, 0)

    def one_image(image, carry):
        tiles = (count_ref[image] + GROUP - 1) // GROUP
        count = far_count_ref[image]
        first = start_ref[image] - count
        qfirst = qstart_ref[image]

        def one_tile(t, carry):
            at = pl.ds(pl.multiple_of((qfirst + t * GROUP) * BS, BS), GROUP * BS)
            query = q_ref[at, :]

            def full(c, state):
                row = pl.ds(pl.multiple_of((first + c * WIDE) * BS, BS), WIDE * BS)
                return fold(state, score(query, keys_ref[row, :]), vals_ref[row, :])

            def rest(state):
                done = count // WIDE * WIDE
                row = pl.ds(pl.multiple_of((first + done) * BS, BS), WIDE * BS)
                spot = lax.broadcasted_iota(jnp.int32, (1, WIDE * BS), 1)
                scores = score(query, keys_ref[row, :])
                scores = jnp.where(spot < (count - done) * BS, scores, neg_large)
                return fold(state, scores, vals_ref[row, :])

            state = (best_ref[at, :][:, :1], accum_ref[at, :])
            state = lax.fori_loop(0, count // WIDE, full, state)
            best, accum = lax.cond(count % WIDE > 0, rest, lambda state: state, state)
            total = jnp.concatenate([accum[:, HD:], accum[:, :HD]], axis=1)
            o_ref[at, :] = accum / total
            return carry

        return lax.fori_loop(0, tiles, one_tile, carry)

    lax.fori_loop(0, images, one_image, 0)

    def emit(j, carry):
        half = BS // 2
        block = o_ref[pl.ds(pl.multiple_of(pos_ref[j] * BS, BS), BS), :].astype(jnp.bfloat16)
        out_ref[j] = jnp.concatenate([block[:half, HD:], block[half:, HD:]], axis=1)
        return carry

    lax.fori_loop(0, out_ref.shape[0], emit, 0)


def project_kernel(
    where_ref, image_ref, got_ref, w0_ref, w1_ref, w2_ref, w3_ref, gate_ref, res_ref, out_ref, mixed_ref
):
    groups = mixed_ref.shape[0]
    heads = mixed_ref.shape[2] // HD
    half = got_ref.shape[1]
    parts = got_ref.shape[0] // (groups * heads)
    for g in range(groups):
        for r in range(parts):
            pieces = [got_ref[(h * parts + r) * groups + g] for h in range(heads)]
            low = r * 2 * half
            mixed_ref[g, low : low + half, :] = jnp.concatenate(
                [piece[:, :HD] for piece in pieces], axis=1
            )
            mixed_ref[g, low + half : low + 2 * half, :] = jnp.concatenate(
                [piece[:, HD:] for piece in pieces], axis=1
            )
    me = where_ref[0]
    total = jnp.dot(mixed_ref[me], w0_ref[...], preferred_element_type=jnp.float32)
    for k, w_ref in ((1, w1_ref), (2, w2_ref), (3, w3_ref)):
        total += jnp.dot(mixed_ref[me ^ k], w_ref[...], preferred_element_type=jnp.float32)
    gating = gate_ref[pl.ds(image_ref[where_ref[1]], 1), :]
    out_ref[...] = (res_ref[...].astype(jnp.float32) + gating * total).astype(jnp.bfloat16)


def by_heads(
    queries, key_rows, values, text_keys, text_values, block_image, gate_image, residual, w_out
):
    tok_blk, ncols = queries.shape
    heads = ncols // HD
    nblk = lax.axis_size("blk")
    nhead = lax.axis_size("head")
    nblocks = block_image.shape[0]
    images = gate_image.shape[0]
    parts = nblk // heads
    blk = lax.axis_index("blk")
    head = lax.axis_index("head")
    smem = pl.BlockSpec(memory_space=pltpu.SMEM)
    vmem = pl.BlockSpec(memory_space=pltpu.VMEM)
    packed = tok_blk + tok_blk // 2
    local = nblocks // parts
    slots = round_up(local, GROUP) + GROUP * images
    groups = [[s * parts + y for s in range(heads)] for y in range(parts)]
    wide_groups = [[b * nhead + x for b in group for x in range(nhead)] for group in groups]
    text_rows = round_up(text_keys.shape[0], 16) + 256
    bf16 = jnp.bfloat16
    w1 = lax.ppermute(w_out, "head", [(i, i ^ 1) for i in range(nhead)])
    w2 = lax.ppermute(w_out, "head", [(i, i ^ 2) for i in range(nhead)])
    w3 = lax.ppermute(w2, "head", [(i, i ^ 1) for i in range(nhead)])
    send, text = pl.pallas_call(
        pack_kernel,
        out_shape=(
            jax.ShapeDtypeStruct((heads, packed, 2 * HD), bf16),
            jax.ShapeDtypeStruct((text_rows, 2 * HD), bf16),
        ),
        in_specs=[smem] + [vmem] * 5,
        out_specs=(vmem, vmem),
        name="pack",
    )((blk // parts).reshape(1), queries, key_rows, values, text_keys, text_values)
    got = lax.all_to_all(
        send, "blk", split_axis=0, concat_axis=0, tiled=True, axis_index_groups=groups
    )
    swap = [(i, i ^ 1) for i in range(nblk)]
    far = lax.ppermute(got[:, :tok_blk], "blk", swap)
    mine = (blk % parts).reshape(1)
    state_shape = (slots * BS, 2 * HD)
    state = pl.pallas_call(
        first_kernel,
        out_shape=(
            jax.ShapeDtypeStruct(state_shape, bf16),
            jax.ShapeDtypeStruct(state_shape, jnp.float32),
            jax.ShapeDtypeStruct(state_shape, jnp.float32),
        ),
        in_specs=[smem, smem, vmem, vmem],
        out_specs=(vmem, vmem, vmem),
        scratch_shapes=[pltpu.VMEM((local * BS, 2 * HD), bf16)] * 2
        + [pltpu.SMEM((images,), jnp.int32)] * 3,
        cost_estimate=pl.CostEstimate(
            flops=8 * HD * local * local * BS * BS,
            transcendentals=local * local * BS * BS,
            bytes_accessed=heads * packed * 4 * HD,
        ),
        name="attend_near",
    )(block_image, mine, got, text)
    key_slots = local + (WIDE - 1) * images + WIDE
    attended = pl.pallas_call(
        second_kernel,
        out_shape=jax.ShapeDtypeStruct((local, BS // 2, 2 * HD), bf16),
        in_specs=[smem, smem] + [vmem] * 5,
        out_specs=vmem,
        scratch_shapes=[pltpu.VMEM((key_slots * BS, 2 * HD), bf16)] * 2
        + [pltpu.VMEM(state_shape, jnp.float32)]
        + [pltpu.SMEM((images,), jnp.int32)] * 5
        + [pltpu.SMEM((local,), jnp.int32)],
        cost_estimate=pl.CostEstimate(
            flops=8 * HD * local * local * BS * BS,
            transcendentals=local * local * BS * BS,
            bytes_accessed=heads * packed * 4 * HD,
        ),
        name="attend_far",
    )(block_image, mine, got, far, *state)
    mixed = lax.all_to_all(
        attended,
        ("blk", "head"),
        split_axis=0,
        concat_axis=0,
        tiled=True,
        axis_index_groups=wide_groups,
    )
    return pl.pallas_call(
        project_kernel,
        out_shape=jax.ShapeDtypeStruct(residual.shape, bf16),
        in_specs=[smem, smem] + [vmem] * 7,
        out_specs=vmem,
        scratch_shapes=[pltpu.VMEM((nhead, BS, ncols), bf16)],
        name="project",
    )(
        jnp.stack([head, blk * nhead + head]),
        block_image,
        mixed,
        w_out,
        w1,
        w2,
        w3,
        gate_image,
        residual,
    )


def solution(mesh):
    placed = (
        P("blk", "head"),
        P("blk", "head"),
        P("blk", "head"),
        P(None, "head"),
        P(None, "head"),
        P(),
        P(),
        P(("blk", "head"), None),
        P("head", None),
    )
    nblk, nhead = mesh.shape["blk"], mesh.shape["head"]

    def step(queries, *others):
        heads = queries.shape[1] // HD
        fits = nhead == 4 and nblk % heads == 0 and nblk == 2 * heads
        fits = fits and queries.shape[0] == nhead * BS
        return (by_heads if fits else on_device)(queries, *others)

    return jax.shard_map(
        step, mesh=mesh, in_specs=placed, out_specs=P(("blk", "head"), None), check_vma=False
    )
```
